768 devices in a mesh: lat: 32 (over y, x), lon: 4 (over z_hi), lev: 6 (over z_lo, core).
Axes of the slice: x: 4, y: 8, z: 12 (z_hi: 4, z_lo: 3; z = z_hi * 3 + z_lo), core: 2. Of those that a mesh axis runs over, the one named last changes fastest.
Arguments:
- gradient: float32 [132, 1024, 1536], P('lev', 'lat', 'lon'), may hold values from -6 to 6
- vertical: float32 [132, 132], replicated, may hold values from -0.5 to 0.5
- variance: float32 [132, 1024, 1536], P('lev', 'lat', 'lon'), may hold values from 0.25 to 4
Outputs:
- increment: float32 [132, 1024, 1536], P('lev', 'lat', 'lon')
The draws below stay inside these ranges and needn't reach their ends.
All inputs are finite; a program needn't handle non-finite values.
Results may differ from the reference program's by a relative error of at most 0.000078.
Values sent between devices are 32-bit elements; how exact they have to be, the bound alone decides.
No kernel may reach another device: no remote copies, remote signals or barrier semaphores. Data moves between devices by JAX's collectives and lax.ppermute only.
A program may use at most 32 MiB of HBM per device.

```python
import math
import jax
import jax.numpy as jnp
from jax import lax

LEV = 132
HALO = 32
LAT = 1024
LON = 1536


def block_scale(own_key, extent, pieces, least, largest):
    def one(position, shards_of):
        heights = jax.random.uniform(jax.random.fold_in(jax.random.fold_in(own_key, 6), position), (shards_of,), jnp.float32, least / len(pieces), largest / len(pieces))
        return jnp.repeat(jnp.exp(heights), extent[position] // shards_of).reshape((-1,) + (1,) * (len(extent) - position - 1))

    gain = one(*pieces[0])
    for cut in pieces[1:]:
        gain = gain * one(*cut)
    return gain


def centred(key, dims, scale, limit, cuts=(), kind=jnp.bfloat16):
    level = block_scale(key, dims, cuts, -0.22, 0.18) if cuts else 1.0
    drawn = jax.random.normal(key, dims, jnp.float32) * scale * level
    return jnp.minimum(jnp.maximum(drawn, -limit), limit).astype(kind)


def setup_inputs(seed: int = 0) -> dict:
    arg_keys = jax.random.split(jax.random.key(seed), 4)
    return {
        "gradient": centred(arg_keys[0], (LEV, LAT, LON), 1.0, 6.0, ((0, 6), (1, 32), (2, 4)), jnp.float32),
        "vertical": centred(arg_keys[1], (LEV, LEV), LEV ** -0.5, 0.5, (), jnp.float32),
        "variance": jnp.clip(jnp.exp(math.log(4.0) - 2.7725887 * jax.random.uniform(arg_keys[2], (LEV, LAT, LON), jnp.float32) ** block_scale(arg_keys[2], (LEV, LAT, LON), ((0, 6), (1, 32), (2, 4)), -0.2, 0.2)), 0.25, 4.0),
    }


def kernel_weights():
    offsets = jnp.arange(-HALO, HALO + 1).astype(jnp.float32)
    bell = jnp.exp(-0.5 * (2.0 * offsets / HALO) ** 2)
    return bell / (jnp.sqrt(jnp.sum(bell)) * jnp.sqrt(jnp.sqrt(jnp.sum(bell * bell))))

def filter_lat(field, weights):
    padded = jnp.pad(field, ((0, 0), (HALO, HALO), (0, 0)))
    rows = field.shape[1]
    total = jnp.zeros_like(field)
    for step in range(2 * HALO + 1):
        total = total + weights[step] * padded[:, step:step + rows, :]
    return total

def filter_lon(field, weights):
    padded = jnp.concatenate([field[:, :, -HALO:], field, field[:, :, :HALO]], axis=2)
    cols = field.shape[2]
    total = jnp.zeros_like(field)
    for step in range(2 * HALO + 1):
        total = total + weights[step] * padded[:, :, step:step + cols]
    return total

def reference(gradient, vertical, variance):
    weights = kernel_weights()
    shape = gradient.shape
    columns = jnp.dot(vertical, gradient.reshape(shape[0], -1), precision=lax.Precision.HIGHEST).reshape(shape)
    smooth = filter_lon(filter_lat(columns, weights), weights)
    scaled = variance * smooth
    return filter_lat(filter_lon(scaled, weights), weights)
```

```python
import math

import jax
import jax.numpy as jnp
from jax import lax
from jax.experimental import pallas as pl
from jax.experimental.pallas import tpu as pltpu
from jax.sharding import PartitionSpec as P


HALO = 32

LEVELS, ROWS, COLS = 22, 32, 384
DEVS = 6
PADDED = 24
TILE = 128
CUTS = 2
PART = LEVELS // CUTS


def tap_scale():
    taps = [math.exp(-0.5 * (2.0 * k / HALO) ** 2) for k in range(-HALO, HALO + 1)]
    return 1.0 / (math.sqrt(sum(taps)) * sum(t * t for t in taps) ** 0.25)


def weights(offset, valid):
    values = jnp.exp(-0.5 * (offset.astype(jnp.float32) * (2.0 / HALO)) ** 2) * tap_scale()
    return jnp.where(valid & (jnp.abs(offset) <= HALO), values, 0.0)


def split_outside(values):
    high = lax.reduce_precision(values, 8, 7)
    return high.astype(jnp.bfloat16), (values - high).astype(jnp.bfloat16)


def split(values):
    high = values.astype(jnp.bfloat16)
    return high, (values - high.astype(jnp.float32)).astype(jnp.bfloat16)


def iota(shape, dim):
    return lax.broadcasted_iota(jnp.int32, shape, dim)


def stored_column(k):
    tile, lane = k // TILE, k % TILE
    low = lane < 64
    edge = jnp.where(low, lane, 256 + lane)
    first = jnp.where(low, 128 + lane, lane)
    second = jnp.where(low, 256 + lane, 128 + lane)
    halo = jnp.where(low, 384 + lane, lane - 128)
    return jnp.where(tile == 0, edge, jnp.where(tile == 1, first, jnp.where(tile == 2, second, halo)))


def wide_column(n):
    m = n - COLS
    column = jnp.where(n < COLS, n, jnp.where(m < 64, n, m - TILE))
    return column, (n < COLS) | (m < HALO) | (m >= TILE - HALO)


def lon_matrices():
    wide = COLS + TILE
    shape = (wide, wide)
    out, valid = wide_column(iota(shape, 1))
    forward = weights(stored_column(iota(shape, 0)) - out, valid)
    shape = (wide, COLS)
    held, valid = wide_column(iota(shape, 0))
    adjoint = weights(held - iota(shape, 1), valid)
    return split_outside(forward) + split_outside(adjoint)


def lat_matrix():
    shape = (ROWS, 3 * ROWS)
    high, low = split_outside(weights(iota(shape, 1) - iota(shape, 0) - ROWS, jnp.full(shape, True)))
    return jnp.concatenate([high, low], axis=0)


def dot(a, b):
    return jnp.dot(a, b, preferred_element_type=jnp.float32)


def exact_right(left, right_high, right_low):
    high, low = split(left)
    return dot(high, right_high) + dot(low, right_high) + dot(high, right_low)


def exact_left(stacked, right):
    rows = stacked.shape[0] // 2
    high, low = split(right)
    both = dot(stacked, high)
    return both[:rows] + both[rows:] + dot(stacked[:rows], low)


def call(body, out_shape, **kwargs):
    return pl.pallas_call(body, out_shape=out_shape, compiler_params=pltpu.CompilerParams(vmem_limit_bytes=48 * 2**20), **kwargs)


def f32(*shape):
    return jax.ShapeDtypeStruct(shape, jnp.float32)


def pack_body(field, out):
    low = iota((LEVELS, 8, TILE), 2) < 64
    for band in range(4):
        t0, t1, t2 = (field[:, 8 * band : 8 * band + 8, TILE * k : TILE * k + TILE] for k in range(3))
        out[band] = jnp.where(low, t0, t2)
        out[4 + band] = jnp.where(low, t1, t0)
        out[8 + band] = jnp.where(low, t2, t1)


def mix_body(matrix, field, out, cells):
    high, low = split(matrix[...])
    cells[...] = jnp.zeros_like(cells)
    for piece in range(DEVS):
        for tile in range(2):
            for row in range(8):
                place = pl.ds((2 * piece + tile) * LEVELS * 8 + row, LEVELS, stride=8)
                cells[PADDED * piece : PADDED * piece + LEVELS, pl.ds((8 * tile + row) * TILE, TILE)] = field[place, :]
    for tile in range(2):
        cells_high, cells_low = split(cells[:, 8 * TILE * tile : 8 * TILE * (tile + 1)])
        mixed = dot(high, cells_high) + dot(low, cells_high) + dot(high, cells_low)
        for piece in range(DEVS):
            for row in range(8):
                place = pl.ds((2 * piece + tile) * LEVELS * 8 + row, LEVELS, stride=8)
                out[place, :] = mixed[PADDED * piece : PADDED * piece + LEVELS, TILE * row : TILE * row + TILE]


def edge_body(matrix, own, above, below, out, to_left, to_right):
    stacked = matrix[...]
    low = iota((16, TILE), 1) < 64
    for level in range(0, LEVELS, 2):
        pair = [
            jnp.concatenate([ref[band, lev] for ref in (above, own, below) for band in range(4)], axis=0)
            for lev in (level, level + 1)
        ]
        done = exact_left(stacked, jnp.concatenate(pair, axis=1))
        for k in range(2):
            edge = done[:, TILE * k : TILE * k + TILE]
            out[level + k] = edge
            top, bottom = edge[:16], pltpu.roll(edge[16:], 64, 1)
            to_left[level + k] = jnp.where(low, top, bottom)
            to_right[level + k] = jnp.where(low, bottom, top)


def inner_body(matrix, own, above, below, out):
    stacked = matrix[...]
    for level in range(LEVELS):
        sides = [
            jnp.concatenate([ref[4 * tile + band, level] for ref in (above, own, below) for band in range(4)], axis=0)
            for tile in range(2)
        ]
        out[level] = exact_left(stacked, jnp.concatenate(sides, axis=1))


def edges_body(field, to_left, to_right):
    group = iota((LEVELS, 8, TILE), 2) // HALO
    left, right = field[:, 0:8, 0:TILE], field[:, 24:32, 2 * TILE :]
    right = pltpu.roll(right, 96, 2)
    for band in range(1, 4):
        left = jnp.where(group == band, pltpu.roll(field[:, 8 * band : 8 * band + 8, 0:TILE], HALO * band, 2), left)
    for band in range(3):
        moved = field[:, 8 * band : 8 * band + 8, 2 * TILE :]
        if band:
            moved = pltpu.roll(moved, HALO * band, 2)
        right = jnp.where(group == (band + 3) % 4, moved, right)
    to_left[...] = left
    to_right[...] = right


def lon_body(edge, inner, from_left, from_right, variance, var_left, var_right, fwd_high, fwd_low, adj_high, adj_low, out):
    flat = (PART * ROWS, TILE)
    low = iota((PART, 16, TILE), 2) < 64
    left, right = from_left[...], from_right[...]
    top = jnp.where(low, right, left)
    bottom = pltpu.roll(jnp.where(low, left, right), 64, 2)
    halo = jnp.concatenate([top, bottom], axis=1).reshape(flat)
    held = jnp.concatenate([edge[...].reshape(flat), inner[...].reshape(PART * ROWS, 2 * TILE), halo], axis=1)
    smooth = exact_right(held, fwd_high[...], fwd_low[...])
    lane = iota((PART, 8, TILE), 2)
    left, right = var_left[...], var_right[...]
    bands = []
    for band in range(4):
        l, r = left, right
        if band:
            l, r = pltpu.roll(left, TILE - HALO * band, 2), pltpu.roll(right, TILE - HALO * band, 2)
        bands.append(jnp.where(lane < HALO, r, jnp.where(lane >= TILE - HALO, l, 0.0)))
    side = jnp.concatenate(bands, axis=1).reshape(flat)
    scale = jnp.concatenate([variance[...].reshape(PART * ROWS, COLS), side], axis=1)
    out[...] = exact_right(smooth * scale, adj_high[...], adj_low[...]).reshape(PART, ROWS, COLS)


def last_body(matrix, *refs):
    stacked = matrix[...]
    out = refs[-1]
    for part in range(CUTS):
        own, above, below = refs[3 * part : 3 * part + 3]
        for level in range(PART):
            cells = jnp.concatenate([above[level], own[level], below[level]], axis=0)
            out[part * PART + level] = exact_left(stacked, cells)


def shifted(cells, axis, step, closed):
    count = lax.axis_size(axis)
    pairs = [(i, (i + step) % count) for i in range(count) if closed or 0 <= i + step < count]
    return lax.ppermute(cells, axis, pairs)


def steps(gradient, vertical, variance):
    lat = lat_matrix()
    lon = lon_matrices()
    tiles = (2 * DEVS, LEVELS, 8, TILE)
    flat = (2 * DEVS * LEVELS * 8, TILE)
    matrix = jnp.pad(vertical.reshape(DEVS, LEVELS, DEVS, LEVELS), ((0, 0), (0, PADDED - LEVELS)) * 2).reshape(DEVS * PADDED, DEVS * PADDED)
    packed = call(pack_body, f32(*tiles))(gradient)
    gathered = lax.all_to_all(packed, "lev", 0, 0, tiled=True)
    scratch = [pltpu.VMEM((DEVS * PADDED, 16 * TILE), jnp.float32)]
    mixed = call(mix_body, f32(*flat), scratch_shapes=scratch)(matrix, gathered.reshape(flat)).reshape(tiles)
    mixed = lax.all_to_all(mixed, "lev", 0, 0, tiled=True)

    edge, inner = mixed[:4], mixed[4:]
    above, below = shifted(edge, "lat", 1, False), shifted(edge, "lat", -1, False)
    inner_above, inner_below = shifted(inner, "lat", 1, False), shifted(inner, "lat", -1, False)

    packed = f32(LEVELS, 16, TILE)
    edge, to_left, to_right = call(edge_body, (f32(LEVELS, ROWS, TILE), packed, packed))(lat, edge, above, below)
    from_left, from_right = shifted(to_right, "lon", 1, True), shifted(to_left, "lon", -1, True)
    var_side = f32(LEVELS, 8, TILE)
    to_left, to_right = call(edges_body, (var_side, var_side))(variance)
    var_left, var_right = shifted(to_right, "lon", 1, True), shifted(to_left, "lon", -1, True)
    inner = call(inner_body, f32(LEVELS, ROWS, 2 * TILE))(lat, inner, inner_above, inner_below)

    operands = []
    for cut in range(CUTS):
        def block(array, cut=cut):
            return pl.BlockSpec((PART,) + array.shape[1:], lambda i: (cut, 0, 0))

        arrays = (edge, inner, from_left, from_right, variance, var_left, var_right)
        specs = [block(a) for a in arrays] + [pl.BlockSpec(m.shape, lambda i: (0, 0)) for m in lon]
        spread = call(
            lon_body, f32(PART, ROWS, COLS), grid=(1,), in_specs=specs,
            out_specs=pl.BlockSpec((PART, ROWS, COLS), lambda i: (0, 0, 0)),
        )(*arrays, *lon)
        operands += [spread, shifted(spread, "lat", 1, False), shifted(spread, "lat", -1, False)]
    return call(last_body, f32(LEVELS, ROWS, COLS))(lat, *operands)


def solution(mesh):
    return jax.shard_map(
        steps,
        mesh=mesh,
        in_specs=(P("lev", "lat", "lon"), P(), P("lev", "lat", "lon")),
        out_specs=P("lev", "lat", "lon"),
        check_vma=False,
    )
```

```python
import math

import jax
import jax.numpy as jnp
from jax import lax
from jax.experimental import pallas as pl
from jax.experimental.pallas import tpu as pltpu
from jax.sharding import PartitionSpec as P


HALO = 32

LEVELS, ROWS, COLS = 22, 32, 384
DEVS = 6
PADDED = 24
TILE = 128


def tap_scale():
    taps = [math.exp(-0.5 * (2.0 * k / HALO) ** 2) for k in range(-HALO, HALO + 1)]
    return 1.0 / (math.sqrt(sum(taps)) * sum(t * t for t in taps) ** 0.25)


def weights(offset, valid):
    values = jnp.exp(-0.5 * (offset.astype(jnp.float32) * (2.0 / HALO)) ** 2) * tap_scale()
    return jnp.where(valid & (jnp.abs(offset) <= HALO), values, 0.0)


def split_outside(values):
    high = lax.reduce_precision(values, 8, 7)
    return high.astype(jnp.bfloat16), (values - high).astype(jnp.bfloat16)


def split(values):
    high = values.astype(jnp.bfloat16)
    return high, (values - high.astype(jnp.float32)).astype(jnp.bfloat16)


def iota(shape, dim):
    return lax.broadcasted_iota(jnp.int32, shape, dim)


def stored_column(k):
    tile, lane = k // TILE, k % TILE
    low = lane < 64
    edge = jnp.where(low, lane, 256 + lane)
    first = jnp.where(low, 128 + lane, lane)
    second = jnp.where(low, 256 + lane, 128 + lane)
    halo = jnp.where(low, 384 + lane, lane - 128)
    return jnp.where(tile == 0, edge, jnp.where(tile == 1, first, jnp.where(tile == 2, second, halo)))


def band(column_in, column_out, valid):
    return split_outside(weights(column_in - column_out, valid))


def inner_matrices():
    shape = (COLS, COLS)
    outer, inner = iota(shape, 0), iota(shape, 1)
    forward = band(stored_column(outer), inner, jnp.full(shape, True))
    shape = (COLS, 2 * TILE)
    outer, inner = iota(shape, 0), iota(shape, 1)
    return forward + band(outer, stored_column(inner + TILE), jnp.full(shape, True))


def edge_column(n):
    m = n - 2 * TILE
    column = jnp.where(n < TILE, n, jnp.where(n < 2 * TILE, n + TILE, jnp.where(m < 64, COLS + m, m - TILE)))
    return column, (m < HALO) | (m >= TILE - HALO)


def edge_matrices():
    shape = (4 * TILE, 3 * TILE)
    column, valid = edge_column(iota(shape, 1))
    forward = band(stored_column(iota(shape, 0)), column, valid)
    shape = (3 * TILE, TILE)
    column, valid = edge_column(iota(shape, 0))
    return forward + band(column, stored_column(iota(shape, 1)), valid)


def lat_matrix():
    shape = (ROWS, 3 * ROWS)
    high, low = split_outside(weights(iota(shape, 1) - iota(shape, 0) - ROWS, jnp.full(shape, True)))
    return jnp.concatenate([high, low], axis=0)


def dot(a, b):
    return jnp.dot(a, b, preferred_element_type=jnp.float32)


def exact_right(left, right_high, right_low):
    high, low = split(left)
    return dot(high, right_high) + dot(low, right_high) + dot(high, right_low)


def exact_left(stacked, right):
    rows = stacked.shape[0] // 2
    high, low = split(right)
    both = dot(stacked, high)
    return both[:rows] + both[rows:] + dot(stacked[:rows], low)


def call(body, out_shape, **kwargs):
    return pl.pallas_call(body, out_shape=out_shape, compiler_params=pltpu.CompilerParams(vmem_limit_bytes=48 * 2**20), **kwargs)


def f32(*shape):
    return jax.ShapeDtypeStruct(shape, jnp.float32)


def pack_body(field, out):
    low = iota((LEVELS, 8, TILE), 2) < 64
    for band in range(4):
        t0, t1, t2 = (field[:, 8 * band : 8 * band + 8, TILE * k : TILE * k + TILE] for k in range(3))
        out[band] = jnp.where(low, t0, t2)
        out[4 + band] = jnp.where(low, t1, t0)
        out[8 + band] = jnp.where(low, t2, t1)


def mix_body(matrix, field, out, cells):
    high, low = split(matrix[...])
    cells[...] = jnp.zeros_like(cells)
    for piece in range(DEVS):
        for tile in range(2):
            for row in range(8):
                place = pl.ds((2 * piece + tile) * LEVELS * 8 + row, LEVELS, stride=8)
                cells[PADDED * piece : PADDED * piece + LEVELS, pl.ds((8 * tile + row) * TILE, TILE)] = field[place, :]
    for tile in range(2):
        cells_high, cells_low = split(cells[:, 8 * TILE * tile : 8 * TILE * (tile + 1)])
        mixed = dot(high, cells_high) + dot(low, cells_high) + dot(high, cells_low)
        for piece in range(DEVS):
            for row in range(8):
                place = pl.ds((2 * piece + tile) * LEVELS * 8 + row, LEVELS, stride=8)
                out[place, :] = mixed[PADDED * piece : PADDED * piece + LEVELS, TILE * row : TILE * row + TILE]


def edge_body(matrix, own, above, below, out, to_left, to_right):
    stacked = matrix[...]
    low = iota((16, TILE), 1) < 64
    for level in range(0, LEVELS, 2):
        pair = [
            jnp.concatenate([ref[band, lev] for ref in (above, own, below) for band in range(4)], axis=0)
            for lev in (level, level + 1)
        ]
        done = exact_left(stacked, jnp.concatenate(pair, axis=1))
        for k in range(2):
            edge = done[:, TILE * k : TILE * k + TILE]
            out[level + k] = edge
            top, bottom = edge[:16], pltpu.roll(edge[16:], 64, 1)
            to_left[level + k] = jnp.where(low, top, bottom)
            to_right[level + k] = jnp.where(low, bottom, top)


def inner_body(matrix, own, above, below, out):
    stacked = matrix[...]
    for level in range(LEVELS):
        sides = [
            jnp.concatenate([ref[4 * tile + band, level] for ref in (above, own, below) for band in range(4)], axis=0)
            for tile in range(2)
        ]
        out[level] = exact_left(stacked, jnp.concatenate(sides, axis=1))


def edges_body(field, to_left, to_right):
    group = iota((LEVELS, 8, TILE), 2) // HALO
    left, right = field[:, 0:8, 0:TILE], field[:, 24:32, 2 * TILE :]
    right = pltpu.roll(right, 96, 2)
    for band in range(1, 4):
        left = jnp.where(group == band, pltpu.roll(field[:, 8 * band : 8 * band + 8, 0:TILE], HALO * band, 2), left)
    for band in range(3):
        moved = field[:, 8 * band : 8 * band + 8, 2 * TILE :]
        if band:
            moved = pltpu.roll(moved, HALO * band, 2)
        right = jnp.where(group == (band + 3) % 4, moved, right)
    to_left[...] = left
    to_right[...] = right


def spread_inner_body(edge, inner, variance, fwd_high, fwd_low, adj_high, adj_low, out):
    count = LEVELS * ROWS
    held = jnp.concatenate([edge[...].reshape(count, TILE), inner[...].reshape(count, 2 * TILE)], axis=1)
    smooth = exact_right(held, fwd_high[...], fwd_low[...])
    scaled = smooth * variance[...].reshape(count, COLS)
    out[...] = exact_right(scaled, adj_high[...], adj_low[...]).reshape(LEVELS, ROWS, 2 * TILE)


def spread_edge_body(edge, inner, from_left, from_right, variance, var_left, var_right, fwd_high, fwd_low, adj_high, adj_low, out):
    flat = (LEVELS * ROWS, TILE)
    low = iota((LEVELS, 16, TILE), 2) < 64
    left, right = from_left[...], from_right[...]
    top = jnp.where(low, right, left)
    bottom = pltpu.roll(jnp.where(low, left, right), 64, 2)
    halo = jnp.concatenate([top, bottom], axis=1).reshape(flat)
    held = jnp.concatenate([edge[...].reshape(flat), inner[...].reshape(LEVELS * ROWS, 2 * TILE), halo], axis=1)
    smooth = exact_right(held, fwd_high[...], fwd_low[...])
    lane = iota((LEVELS, 8, TILE), 2)
    left, right = var_left[...], var_right[...]
    bands = []
    for band in range(4):
        l, r = left, right
        if band:
            l, r = pltpu.roll(left, TILE - HALO * band, 2), pltpu.roll(right, TILE - HALO * band, 2)
        bands.append(jnp.where(lane < HALO, r, jnp.where(lane >= TILE - HALO, l, 0.0)))
    side = jnp.concatenate(bands, axis=1).reshape(flat)
    first, last = variance[:, :, :TILE].reshape(flat), variance[:, :, 2 * TILE :].reshape(flat)
    scaled = smooth * jnp.concatenate([first, last, side], axis=1)
    out[...] = exact_right(scaled, adj_high[...], adj_low[...]).reshape(LEVELS, ROWS, TILE)


def last_inner_body(matrix, own, above, below, out):
    stacked = matrix[...]
    for level in range(LEVELS):
        out[level] = exact_left(stacked, jnp.concatenate([above[level], own[level], below[level]], axis=0))


def last_edge_body(matrix, own, above, below, inner, out):
    stacked = matrix[...]
    low = iota((ROWS, TILE), 1) < 64
    for level in range(0, LEVELS, 2):
        pair = [jnp.concatenate([above[k], own[k], below[k]], axis=0) for k in (level, level + 1)]
        done = exact_left(stacked, jnp.concatenate(pair, axis=1))
        for k in range(2):
            edge = done[:, TILE * k : TILE * k + TILE]
            first, second = inner[level + k, :, :TILE], inner[level + k, :, TILE:]
            out[level + k, :, :TILE] = jnp.where(low, edge, first)
            out[level + k, :, TILE : 2 * TILE] = jnp.where(low, first, second)
            out[level + k, :, 2 * TILE :] = jnp.where(low, second, edge)


def shifted(cells, axis, step, closed):
    count = lax.axis_size(axis)
    pairs = [(i, (i + step) % count) for i in range(count) if closed or 0 <= i + step < count]
    return lax.ppermute(cells, axis, pairs)


def steps(gradient, vertical, variance):
    lat = lat_matrix()
    tiles = (2 * DEVS, LEVELS, 8, TILE)
    flat = (2 * DEVS * LEVELS * 8, TILE)
    matrix = jnp.pad(vertical.reshape(DEVS, LEVELS, DEVS, LEVELS), ((0, 0), (0, PADDED - LEVELS)) * 2).reshape(DEVS * PADDED, DEVS * PADDED)
    packed = call(pack_body, f32(*tiles))(gradient)
    gathered = lax.all_to_all(packed, "lev", 0, 0, tiled=True)
    scratch = [pltpu.VMEM((DEVS * PADDED, 16 * TILE), jnp.float32)]
    mixed = call(mix_body, f32(*flat), scratch_shapes=scratch)(matrix, gathered.reshape(flat)).reshape(tiles)
    mixed = lax.all_to_all(mixed, "lev", 0, 0, tiled=True)

    edge, inner = mixed[:4], mixed[4:]
    above, below = shifted(edge, "lat", 1, False), shifted(edge, "lat", -1, False)
    inner_above, inner_below = shifted(inner, "lat", 1, False), shifted(inner, "lat", -1, False)

    packed = f32(LEVELS, 16, TILE)
    edge, to_left, to_right = call(edge_body, (f32(LEVELS, ROWS, TILE), packed, packed))(lat, edge, above, below)
    from_left, from_right = shifted(to_right, "lon", 1, True), shifted(to_left, "lon", -1, True)
    var_side = f32(LEVELS, 8, TILE)
    to_left, to_right = call(edges_body, (var_side, var_side))(variance)
    var_left, var_right = shifted(to_right, "lon", 1, True), shifted(to_left, "lon", -1, True)
    inner = call(inner_body, f32(LEVELS, ROWS, 2 * TILE))(lat, inner, inner_above, inner_below)

    back = call(spread_inner_body, f32(LEVELS, ROWS, 2 * TILE))(edge, inner, variance, *inner_matrices())
    back_above, back_below = shifted(back, "lat", 1, False), shifted(back, "lat", -1, False)
    sides = (from_left, from_right, variance, var_left, var_right)
    rim = call(spread_edge_body, f32(LEVELS, ROWS, TILE))(edge, inner, *sides, *edge_matrices())
    rim_above, rim_below = shifted(rim, "lat", 1, False), shifted(rim, "lat", -1, False)
    back = call(last_inner_body, f32(LEVELS, ROWS, 2 * TILE))(lat, back, back_above, back_below)
    return call(last_edge_body, f32(LEVELS, ROWS, COLS))(lat, rim, rim_above, rim_below, back)


def solution(mesh):
    return jax.shard_map(
        steps,
        mesh=mesh,
        in_specs=(P("lev", "lat", "lon"), P(), P("lev", "lat", "lon")),
        out_specs=P("lev", "lat", "lon"),
        check_vma=False,
    )
```

```python
import math

import jax
import jax.numpy as jnp
from jax import lax
from jax.experimental import pallas as pl
from jax.experimental.pallas import tpu as pltpu
from jax.sharding import PartitionSpec as P


HALO = 32

LEVELS, ROWS, COLS = 22, 32, 384
DEVS = 6
PADDED = 24
TILE = 128


def tap_scale():
    taps = [math.exp(-0.5 * (2.0 * k / HALO) ** 2) for k in range(-HALO, HALO + 1)]
    return 1.0 / (math.sqrt(sum(taps)) * sum(t * t for t in taps) ** 0.25)


def weights(offset, valid):
    values = jnp.exp(-0.5 * (offset.astype(jnp.float32) * (2.0 / HALO)) ** 2) * tap_scale()
    return jnp.where(valid, values, 0.0)


def split(values):
    high = values.astype(jnp.bfloat16)
    return high, (values - high.astype(jnp.float32)).astype(jnp.bfloat16)


def iota(shape, dim):
    return lax.broadcasted_iota(jnp.int32, shape, dim)


def stored_column(k):
    tile, lane = k >> 7, k & (TILE - 1)
    low = lane < 64
    edge = jnp.where(low, lane, 256 + lane)
    first = jnp.where(low, 128 + lane, lane)
    second = jnp.where(low, 256 + lane, 128 + lane)
    halo = jnp.where(low, 384 + lane, lane - 128)
    return jnp.where(tile == 0, edge, jnp.where(tile == 1, first, jnp.where(tile == 2, second, halo)))


def edge_column(n):
    m = n - 2 * TILE
    column = jnp.where(n < TILE, n, jnp.where(n < 2 * TILE, n + TILE, jnp.where(m < 64, COLS + m, m - TILE)))
    return column, (m < HALO) | (m >= TILE - HALO)


MATRICES = ((COLS, COLS), (COLS, 2 * TILE), (4 * TILE, 3 * TILE), (3 * TILE, TILE))


def matrices_body(lat, *outs):
    shape = (ROWS, 3 * ROWS)
    offset = iota(shape, 1) - iota(shape, 0) - ROWS
    lat[...] = jnp.concatenate(split(weights(offset, jnp.abs(offset) <= HALO)), axis=0)
    for kind, shape in enumerate(MATRICES):
        outer, inner = iota(shape, 0), iota(shape, 1)
        valid = True
        if kind == 0:
            offset = stored_column(outer) - inner
        elif kind == 1:
            offset = outer - stored_column(inner + TILE)
        elif kind == 2:
            column, valid = edge_column(inner)
            offset = stored_column(outer) - column
        else:
            column, valid = edge_column(outer)
            offset = column - stored_column(inner)
        outs[2 * kind][...], outs[2 * kind + 1][...] = split(weights(offset, (jnp.abs(offset) <= HALO) & valid))


def dot(a, b):
    return jnp.dot(a, b, preferred_element_type=jnp.float32)


def exact_right(left, right_high, right_low):
    high, low = split(left)
    return dot(high, right_high) + dot(low, right_high) + dot(high, right_low)


def exact_left(stacked, right):
    rows = stacked.shape[0] // 2
    high, low = split(right)
    both = dot(stacked, high)
    return both[:rows] + both[rows:] + dot(stacked[:rows], low)


def call(body, out_shape, **kwargs):
    return pl.pallas_call(body, out_shape=out_shape, compiler_params=pltpu.CompilerParams(vmem_limit_bytes=20 * 2**20), **kwargs)


def f32(*shape):
    return jax.ShapeDtypeStruct(shape, jnp.float32)


def pack_body(field, out):
    low = iota((LEVELS, 8, TILE), 2) < 64
    for band in range(4):
        t0, t1, t2 = (field[:, 8 * band : 8 * band + 8, TILE * k : TILE * k + TILE] for k in range(3))
        tiles = (jnp.where(low, t0, t2), jnp.where(low, t1, t0), jnp.where(low, t2, t1))
        for kind in range(3):
            half, dev = divmod(4 * kind + band, DEVS)
            out[2 * dev + half] = tiles[kind]


def mix_half(half):
    def body(matrix, field, out, cells):
        high, low = split(matrix[...])
        cells[...] = jnp.zeros_like(cells)
        for piece in range(DEVS):
            for row in range(8):
                place = pl.ds((2 * piece + half) * LEVELS * 8 + row, LEVELS, stride=8)
                cells[PADDED * piece : PADDED * piece + LEVELS, TILE * row : TILE * row + TILE] = field[place, :]
        cells_high, cells_low = split(cells[...])
        mixed = dot(high, cells_high) + dot(low, cells_high) + dot(high, cells_low)
        for piece in range(DEVS):
            for row in range(8):
                place = pl.ds(piece * LEVELS * 8 + row, LEVELS, stride=8)
                out[place, :] = mixed[PADDED * piece : PADDED * piece + LEVELS, TILE * row : TILE * row + TILE]

    return body


def edge_body(matrix, own, above, below, out, to_left, to_right):
    stacked = matrix[...]
    low = iota((16, TILE), 1) < 64
    for level in range(0, LEVELS, 2):
        pair = [
            jnp.concatenate([ref[band, lev] for ref in (above, own, below) for band in range(4)], axis=0)
            for lev in (level, level + 1)
        ]
        done = exact_left(stacked, jnp.concatenate(pair, axis=1))
        for k in range(2):
            edge = done[:, TILE * k : TILE * k + TILE]
            out[level + k] = edge
            top, bottom = edge[:16], pltpu.roll(edge[16:], 64, 1)
            to_left[level + k] = jnp.where(low, top, bottom)
            to_right[level + k] = jnp.where(low, bottom, top)


def inner_body(matrix, *refs):
    stacked, out = matrix[...], refs[-1]
    early, late = refs[:3], refs[3:6]

    def column(side, tile, level):
        places = [4 * (tile + 1) + band for band in range(4)]
        return [early[side][p, level] if p < DEVS else late[side][p - DEVS, level] for p in places]

    for level in range(LEVELS):
        sides = [jnp.concatenate([c for side in (1, 0, 2) for c in column(side, tile, level)], axis=0) for tile in range(2)]
        out[level] = exact_left(stacked, jnp.concatenate(sides, axis=1))


def edges_body(field, to_left, to_right):
    group = iota((LEVELS, 8, TILE), 2) // HALO
    left, right = field[:, 0:8, 0:TILE], field[:, 24:32, 2 * TILE :]
    right = pltpu.roll(right, 96, 2)
    for band in range(1, 4):
        left = jnp.where(group == band, pltpu.roll(field[:, 8 * band : 8 * band + 8, 0:TILE], HALO * band, 2), left)
    for band in range(3):
        moved = field[:, 8 * band : 8 * band + 8, 2 * TILE :]
        if band:
            moved = pltpu.roll(moved, HALO * band, 2)
        right = jnp.where(group == (band + 3) % 4, moved, right)
    to_left[...] = left
    to_right[...] = right


def spread_inner_body(edge, inner, variance, fwd_high, fwd_low, adj_high, adj_low, out):
    count = LEVELS * ROWS
    held = jnp.concatenate([edge[...].reshape(count, TILE), inner[...].reshape(count, 2 * TILE)], axis=1)
    smooth = exact_right(held, fwd_high[...], fwd_low[...])
    scaled = smooth * variance[...].reshape(count, COLS)
    out[...] = exact_right(scaled, adj_high[...], adj_low[...]).reshape(LEVELS, ROWS, 2 * TILE)


def spread_edge_body(edge, inner, from_left, from_right, variance, var_left, var_right, fwd_high, fwd_low, adj_high, adj_low, out):
    flat = (LEVELS * ROWS, TILE)
    low = iota((LEVELS, 16, TILE), 2) < 64
    left, right = from_left[...], from_right[...]
    top = jnp.where(low, right, left)
    bottom = pltpu.roll(jnp.where(low, left, right), 64, 2)
    halo = jnp.concatenate([top, bottom], axis=1).reshape(flat)
    held = jnp.concatenate([edge[...].reshape(flat), inner[...].reshape(LEVELS * ROWS, 2 * TILE), halo], axis=1)
    smooth = exact_right(held, fwd_high[...], fwd_low[...])
    lane = iota((LEVELS, 8, TILE), 2)
    left, right = var_left[...], var_right[...]
    bands = []
    for band in range(4):
        l, r = left, right
        if band:
            l, r = pltpu.roll(left, TILE - HALO * band, 2), pltpu.roll(right, TILE - HALO * band, 2)
        bands.append(jnp.where(lane < HALO, r, jnp.where(lane >= TILE - HALO, l, 0.0)))
    side = jnp.concatenate(bands, axis=1).reshape(flat)
    first, last = variance[:, :, :TILE].reshape(flat), variance[:, :, 2 * TILE :].reshape(flat)
    scaled = smooth * jnp.concatenate([first, last, side], axis=1)
    out[...] = exact_right(scaled, adj_high[...], adj_low[...]).reshape(LEVELS, ROWS, TILE)


def last_inner_body(matrix, own, above, below, out):
    stacked = matrix[...]
    for level in range(LEVELS):
        out[level] = exact_left(stacked, jnp.concatenate([above[level], own[level], below[level]], axis=0))


def last_edge_body(matrix, own, above, below, inner, out):
    stacked = matrix[...]
    low = iota((ROWS, TILE), 1) < 64
    for level in range(0, LEVELS, 2):
        pair = [jnp.concatenate([above[k], own[k], below[k]], axis=0) for k in (level, level + 1)]
        done = exact_left(stacked, jnp.concatenate(pair, axis=1))
        for k in range(2):
            edge = done[:, TILE * k : TILE * k + TILE]
            first, second = inner[level + k, :, :TILE], inner[level + k, :, TILE:]
            out[level + k, :, :TILE] = jnp.where(low, edge, first)
            out[level + k, :, TILE : 2 * TILE] = jnp.where(low, first, second)
            out[level + k, :, 2 * TILE :] = jnp.where(low, second, edge)


def shifted(cells, axis, step, closed):
    count = lax.axis_size(axis)
    pairs = [(i, (i + step) % count) for i in range(count) if closed or 0 <= i + step < count]
    return lax.ppermute(cells, axis, pairs)


def steps(gradient, vertical, variance):
    shapes = [(2 * ROWS, 3 * ROWS)] + [shape for shape in MATRICES for _ in range(2)]
    lat, *bands = call(matrices_body, [jax.ShapeDtypeStruct(shape, jnp.bfloat16) for shape in shapes])()
    tiles = (2 * DEVS, LEVELS, 8, TILE)
    flat = (2 * DEVS * LEVELS * 8, TILE)
    matrix = jnp.pad(vertical.reshape(DEVS, LEVELS, DEVS, LEVELS), ((0, 0), (0, PADDED - LEVELS)) * 2).reshape(DEVS * PADDED, DEVS * PADDED)
    packed = call(pack_body, f32(*tiles))(gradient)
    gathered = lax.all_to_all(packed, "lev", 0, 0, tiled=True)
    scratch = [pltpu.VMEM((DEVS * PADDED, 8 * TILE), jnp.float32)]
    halves = []
    for half in range(2):
        mixed = call(mix_half(half), f32(flat[0] // 2, TILE), scratch_shapes=scratch)(matrix, gathered.reshape(flat))
        own = lax.all_to_all(mixed.reshape(DEVS, LEVELS, 8, TILE), "lev", 0, 0, tiled=True)
        halves.append((own, shifted(own, "lat", 1, False), shifted(own, "lat", -1, False)))
    early, late = halves

    packed = f32(LEVELS, 16, TILE)
    edge, to_left, to_right = call(edge_body, (f32(LEVELS, ROWS, TILE), packed, packed))(lat, *early)
    from_left, from_right = shifted(to_right, "lon", 1, True), shifted(to_left, "lon", -1, True)
    var_side = f32(LEVELS, 8, TILE)
    to_left, to_right = call(edges_body, (var_side, var_side))(variance)
    var_left, var_right = shifted(to_right, "lon", 1, True), shifted(to_left, "lon", -1, True)
    inner = call(inner_body, f32(LEVELS, ROWS, 2 * TILE))(lat, *early, *late)

    back = call(spread_inner_body, f32(LEVELS, ROWS, 2 * TILE))(edge, inner, variance, *bands[:4])
    back_above, back_below = shifted(back, "lat", 1, False), shifted(back, "lat", -1, False)
    sides = (from_left, from_right, variance, var_left, var_right)
    rim = call(spread_edge_body, f32(LEVELS, ROWS, TILE))(edge, inner, *sides, *bands[4:])
    rim_above, rim_below = shifted(rim, "lat", 1, False), shifted(rim, "lat", -1, False)
    back = call(last_inner_body, f32(LEVELS, ROWS, 2 * TILE))(lat, back, back_above, back_below)
    return call(last_edge_body, f32(LEVELS, ROWS, COLS))(lat, rim, rim_above, rim_below, back)


def solution(mesh):
    return jax.shard_map(
        steps,
        mesh=mesh,
        in_specs=(P("lev", "lat", "lon"), P(), P("lev", "lat", "lon")),
        out_specs=P("lev", "lat", "lon"),
        check_vma=False,
    )
```

```python
import math

import jax
import jax.numpy as jnp
from jax import lax
from jax.experimental import pallas as pl
from jax.experimental.pallas import tpu as pltpu
from jax.sharding import PartitionSpec as P


HALO = 32

LEVELS, ROWS, COLS = 22, 32, 384
DEVS = 6
PADDED = 24
TILE = 128
CUTS = 2
PART = LEVELS // CUTS


def tap_scale():
    taps = [math.exp(-0.5 * (2.0 * k / HALO) ** 2) for k in range(-HALO, HALO + 1)]
    return 1.0 / (math.sqrt(sum(taps)) * sum(t * t for t in taps) ** 0.25)


def weights(offset, valid):
    values = jnp.exp(-0.5 * (offset.astype(jnp.float32) * (2.0 / HALO)) ** 2) * tap_scale()
    return jnp.where(valid, values, 0.0)


def split(values):
    high = values.astype(jnp.bfloat16)
    return high, (values - high.astype(jnp.float32)).astype(jnp.bfloat16)


def iota(shape, dim):
    return lax.broadcasted_iota(jnp.int32, shape, dim)


def stored_column(k):
    tile, lane = k >> 7, k & (TILE - 1)
    low = lane < 64
    edge = jnp.where(low, lane, 256 + lane)
    first = jnp.where(low, 128 + lane, lane)
    second = jnp.where(low, 256 + lane, 128 + lane)
    halo = jnp.where(low, 384 + lane, lane - 128)
    return jnp.where(tile == 0, edge, jnp.where(tile == 1, first, jnp.where(tile == 2, second, halo)))


def edge_column(n):
    m = n - 2 * TILE
    column = jnp.where(n < TILE, n, jnp.where(n < 2 * TILE, n + TILE, jnp.where(m < 64, COLS + m, m - TILE)))
    return column, (m < HALO) | (m >= TILE - HALO)


MATRICES = ((COLS, COLS), (COLS, 2 * TILE), (4 * TILE, 3 * TILE), (3 * TILE, TILE))


def matrices_body(lat, *outs):
    shape = (ROWS, 3 * ROWS)
    offset = iota(shape, 1) - iota(shape, 0) - ROWS
    lat[...] = jnp.concatenate(split(weights(offset, jnp.abs(offset) <= HALO)), axis=0)
    for kind, shape in enumerate(MATRICES):
        outer, inner = iota(shape, 0), iota(shape, 1)
        valid = True
        if kind == 0:
            offset = stored_column(outer) - inner
        elif kind == 1:
            offset = outer - stored_column(inner + TILE)
        elif kind == 2:
            column, valid = edge_column(inner)
            offset = stored_column(outer) - column
        else:
            column, valid = edge_column(outer)
            offset = column - stored_column(inner)
        outs[2 * kind][...], outs[2 * kind + 1][...] = split(weights(offset, (jnp.abs(offset) <= HALO) & valid))


def dot(a, b):
    return jnp.dot(a, b, preferred_element_type=jnp.float32)


def exact_right(left, right_high, right_low):
    high, low = split(left)
    return dot(high, right_high) + dot(low, right_high) + dot(high, right_low)


def exact_left(stacked, right):
    rows = stacked.shape[0] // 2
    high, low = split(right)
    both = dot(stacked, high)
    return both[:rows] + both[rows:] + dot(stacked[:rows], low)


def call(body, out_shape, **kwargs):
    return pl.pallas_call(body, out_shape=out_shape, compiler_params=pltpu.CompilerParams(vmem_limit_bytes=20 * 2**20), **kwargs)


def f32(*shape):
    return jax.ShapeDtypeStruct(shape, jnp.float32)


def pack_body(field, out):
    low = iota((LEVELS, 8, TILE), 2) < 64
    for band in range(4):
        t0, t1, t2 = (field[:, 8 * band : 8 * band + 8, TILE * k : TILE * k + TILE] for k in range(3))
        tiles = (jnp.where(low, t0, t2), jnp.where(low, t1, t0), jnp.where(low, t2, t1))
        for kind in range(3):
            half, dev = divmod(4 * kind + band, DEVS)
            out[2 * dev + half] = tiles[kind]


def mix_half(half):
    def body(matrix, field, out, cells):
        high, low = split(matrix[...])
        cells[...] = jnp.zeros_like(cells)
        for piece in range(DEVS):
            for row in range(8):
                place = pl.ds((2 * piece + half) * LEVELS * 8 + row, LEVELS, stride=8)
                cells[PADDED * piece : PADDED * piece + LEVELS, TILE * row : TILE * row + TILE] = field[place, :]
        cells_high, cells_low = split(cells[...])
        mixed = dot(high, cells_high) + dot(low, cells_high) + dot(high, cells_low)
        for piece in range(DEVS):
            for row in range(8):
                place = pl.ds(piece * LEVELS * 8 + row, LEVELS, stride=8)
                out[place, :] = mixed[PADDED * piece : PADDED * piece + LEVELS, TILE * row : TILE * row + TILE]

    return body


def edge_body(matrix, own, above, below, out, to_left, to_right):
    stacked = matrix[...]
    low = iota((16, TILE), 1) < 64
    for level in range(0, LEVELS, 2):
        pair = [
            jnp.concatenate([ref[band, lev] for ref in (above, own, below) for band in range(4)], axis=0)
            for lev in (level, level + 1)
        ]
        done = exact_left(stacked, jnp.concatenate(pair, axis=1))
        for k in range(2):
            edge = done[:, TILE * k : TILE * k + TILE]
            out[level + k] = edge
            top, bottom = edge[:16], pltpu.roll(edge[16:], 64, 1)
            to_left[level + k] = jnp.where(low, top, bottom)
            to_right[level + k] = jnp.where(low, bottom, top)


def inner_body(matrix, *refs):
    stacked, out = matrix[...], refs[-1]
    early, late = refs[:3], refs[3:6]

    def column(side, tile, level):
        places = [4 * (tile + 1) + band for band in range(4)]
        return [early[side][p, level] if p < DEVS else late[side][p - DEVS, level] for p in places]

    for level in range(LEVELS):
        sides = [jnp.concatenate([c for side in (1, 0, 2) for c in column(side, tile, level)], axis=0) for tile in range(2)]
        out[level] = exact_left(stacked, jnp.concatenate(sides, axis=1))


def edges_body(field, to_left, to_right):
    group = iota((LEVELS, 8, TILE), 2) // HALO
    left, right = field[:, 0:8, 0:TILE], field[:, 24:32, 2 * TILE :]
    right = pltpu.roll(right, 96, 2)
    for band in range(1, 4):
        left = jnp.where(group == band, pltpu.roll(field[:, 8 * band : 8 * band + 8, 0:TILE], HALO * band, 2), left)
    for band in range(3):
        moved = field[:, 8 * band : 8 * band + 8, 2 * TILE :]
        if band:
            moved = pltpu.roll(moved, HALO * band, 2)
        right = jnp.where(group == (band + 3) % 4, moved, right)
    to_left[...] = left
    to_right[...] = right


def spread_inner_body(edge, inner, variance, fwd_high, fwd_low, adj_high, adj_low, out):
    count = PART * ROWS
    held = jnp.concatenate([edge[...].reshape(count, TILE), inner[...].reshape(count, 2 * TILE)], axis=1)
    smooth = exact_right(held, fwd_high[...], fwd_low[...])
    scaled = smooth * variance[...].reshape(count, COLS)
    out[...] = exact_right(scaled, adj_high[...], adj_low[...]).reshape(PART, ROWS, 2 * TILE)


def spread_edge_body(edge, inner, from_left, from_right, variance, var_left, var_right, fwd_high, fwd_low, adj_high, adj_low, out):
    flat = (LEVELS * ROWS, TILE)
    low = iota((LEVELS, 16, TILE), 2) < 64
    left, right = from_left[...], from_right[...]
    top = jnp.where(low, right, left)
    bottom = pltpu.roll(jnp.where(low, left, right), 64, 2)
    halo = jnp.concatenate([top, bottom], axis=1).reshape(flat)
    held = jnp.concatenate([edge[...].reshape(flat), inner[...].reshape(LEVELS * ROWS, 2 * TILE), halo], axis=1)
    smooth = exact_right(held, fwd_high[...], fwd_low[...])
    lane = iota((LEVELS, 8, TILE), 2)
    left, right = var_left[...], var_right[...]
    bands = []
    for band in range(4):
        l, r = left, right
        if band:
            l, r = pltpu.roll(left, TILE - HALO * band, 2), pltpu.roll(right, TILE - HALO * band, 2)
        bands.append(jnp.where(lane < HALO, r, jnp.where(lane >= TILE - HALO, l, 0.0)))
    side = jnp.concatenate(bands, axis=1).reshape(flat)
    first, last = variance[:, :, :TILE].reshape(flat), variance[:, :, 2 * TILE :].reshape(flat)
    scaled = smooth * jnp.concatenate([first, last, side], axis=1)
    out[...] = exact_right(scaled, adj_high[...], adj_low[...]).reshape(LEVELS, ROWS, TILE)


def last_inner_body(matrix, *refs):
    stacked, out = matrix[...], refs[-1]
    for cut in range(CUTS):
        own, above, below = refs[3 * cut : 3 * cut + 3]
        for level in range(PART):
            cells = jnp.concatenate([above[level], own[level], below[level]], axis=0)
            out[PART * cut + level] = exact_left(stacked, cells)


def last_edge_body(matrix, own, above, below, inner, out):
    stacked = matrix[...]
    low = iota((ROWS, TILE), 1) < 64
    for level in range(0, LEVELS, 2):
        pair = [jnp.concatenate([above[k], own[k], below[k]], axis=0) for k in (level, level + 1)]
        done = exact_left(stacked, jnp.concatenate(pair, axis=1))
        for k in range(2):
            edge = done[:, TILE * k : TILE * k + TILE]
            first, second = inner[level + k, :, :TILE], inner[level + k, :, TILE:]
            out[level + k, :, :TILE] = jnp.where(low, edge, first)
            out[level + k, :, TILE : 2 * TILE] = jnp.where(low, first, second)
            out[level + k, :, 2 * TILE :] = jnp.where(low, second, edge)


def shifted(cells, axis, step, closed):
    count = lax.axis_size(axis)
    pairs = [(i, (i + step) % count) for i in range(count) if closed or 0 <= i + step < count]
    return lax.ppermute(cells, axis, pairs)


def steps(gradient, vertical, variance):
    shapes = [(2 * ROWS, 3 * ROWS)] + [shape for shape in MATRICES for _ in range(2)]
    lat, *bands = call(matrices_body, [jax.ShapeDtypeStruct(shape, jnp.bfloat16) for shape in shapes])()
    tiles = (2 * DEVS, LEVELS, 8, TILE)
    flat = (2 * DEVS * LEVELS * 8, TILE)
    matrix = jnp.pad(vertical.reshape(DEVS, LEVELS, DEVS, LEVELS), ((0, 0), (0, PADDED - LEVELS)) * 2).reshape(DEVS * PADDED, DEVS * PADDED)
    packed = call(pack_body, f32(*tiles))(gradient)
    gathered = lax.all_to_all(packed, "lev", 0, 0, tiled=True)
    scratch = [pltpu.VMEM((DEVS * PADDED, 8 * TILE), jnp.float32)]
    halves = []
    for half in range(2):
        mixed = call(mix_half(half), f32(flat[0] // 2, TILE), scratch_shapes=scratch)(matrix, gathered.reshape(flat))
        own = lax.all_to_all(mixed.reshape(DEVS, LEVELS, 8, TILE), "lev", 0, 0, tiled=True)
        halves.append((own, shifted(own, "lat", 1, False), shifted(own, "lat", -1, False)))
    early, late = halves

    packed = f32(LEVELS, 16, TILE)
    edge, to_left, to_right = call(edge_body, (f32(LEVELS, ROWS, TILE), packed, packed))(lat, *early)
    from_left, from_right = shifted(to_right, "lon", 1, True), shifted(to_left, "lon", -1, True)
    var_side = f32(LEVELS, 8, TILE)
    to_left, to_right = call(edges_body, (var_side, var_side))(variance)
    var_left, var_right = shifted(to_right, "lon", 1, True), shifted(to_left, "lon", -1, True)
    inner = call(inner_body, f32(LEVELS, ROWS, 2 * TILE))(lat, *early, *late)

    backs = []
    for cut in range(CUTS):

        def block(array, cut=cut):
            return pl.BlockSpec((PART,) + array.shape[1:], lambda i: (cut, 0, 0))

        arrays = (edge, inner, variance)
        specs = [block(array) for array in arrays] + [pl.BlockSpec(m.shape, lambda i: (0, 0)) for m in bands[:4]]
        shape = (PART, ROWS, 2 * TILE)
        own = call(spread_inner_body, f32(*shape), grid=(1,), in_specs=specs, out_specs=pl.BlockSpec(shape, lambda i: (0, 0, 0)))(*arrays, *bands[:4])
        backs += [own, shifted(own, "lat", 1, False), shifted(own, "lat", -1, False)]
    sides = (from_left, from_right, variance, var_left, var_right)
    rim = call(spread_edge_body, f32(LEVELS, ROWS, TILE))(edge, inner, *sides, *bands[4:])
    rim_above, rim_below = shifted(rim, "lat", 1, False), shifted(rim, "lat", -1, False)
    back = call(last_inner_body, f32(LEVELS, ROWS, 2 * TILE))(lat, *backs)
    return call(last_edge_body, f32(LEVELS, ROWS, COLS))(lat, rim, rim_above, rim_below, back)


def solution(mesh):
    return jax.shard_map(
        steps,
        mesh=mesh,
        in_specs=(P("lev", "lat", "lon"), P(), P("lev", "lat", "lon")),
        out_specs=P("lev", "lat", "lon"),
        check_vma=False,
    )
```
